768 devices in a mesh: row: 48 (over y_lo, z), col: 16 (over y_hi, x, core).
Axes of the slice: x: 4, y: 8 (y_hi: 2, y_lo: 4; y = y_hi * 4 + y_lo), z: 12, core: 2. Of those that a mesh axis runs over, the one named last changes fastest.
Arguments:
- object_field: float32 [2, 18432, 4096], P(None, 'row', 'col'), may hold values from -3 to 3
- probe_field: float32 [2, 256, 256], replicated, may hold values from -6 to 6
- amplitudes: bfloat16 [48, 16, 4, 256, 256], P('row', 'col'), may hold values from 0.5 to 16
- pos_rows: int32 [48, 16, 4], P('row', 'col'), may hold values from 0 to 383
- pos_cols: int32 [48, 16, 4], P('row', 'col'), may hold values from 0 to 255
- scan_pick: int32 [48, 16, 2], P('row', 'col'), may hold values from 0 to 3
- scan_count: int32 [768], P(('row', 'col')), may hold values from 1 to 2, 1152 in all
Outputs:
- object_next: float32 [2, 18432, 4096], P(None, 'row', 'col')
- probe_next: float32 [2, 256, 256], replicated
The draws below stay inside these ranges and needn't reach their ends.
Inputs may be any that keep to these rules, and one draw needn't show every extreme that they name: `scan_count`: each tile's list has 1 to 2 scans; the longest list has exactly 2; lists total 1152 scans.
All inputs are finite; a program needn't handle non-finite values. No bound on the sum of `scan_count` on one device may be relied on, other than what follows from the above.
Results may differ from the reference program's by a relative error of at most 0.0003.
Values sent between devices are 32-bit elements; how exact they have to be, the bound alone decides.
No kernel may reach another device: no remote copies, remote signals or barrier semaphores. Data moves between devices by JAX's collectives and lax.ppermute only.
A program may use at most 64 MiB of HBM per device.

```python
import math
import jax
import jax.numpy as jnp
import numpy as np
from jax import lax

PW = 256
TH = 384
TW = 256
SCAP = 2
POOL = 4
NH = 18432
NW = 4096
TILES = 768
USED = 1152
N_ROW = 48
N_COL = 16


def touch_ends(array, stream_key, smallest, largest):
    shape = array.shape
    index_at = [jax.random.randint(jax.random.fold_in(stream_key, axis), (), 0, shape[axis]) for axis in range(len(shape))]
    array = array.at[tuple(index_at)].set(smallest)
    longest = shape.index(max(shape))
    index_at[longest] = (index_at[longest] + 1) % shape[longest]
    return array.at[tuple(index_at)].set(largest)


def block_scale(key, dims, shards, low, largest):
    loudness = 1.0
    for position, parts in shards:
        heights = jax.random.uniform(jax.random.fold_in(jax.random.fold_in(key, 6), position), (parts,), jnp.float32, low / len(shards), largest / len(shards))
        loudness = loudness * jnp.repeat(jnp.exp(heights), dims[position] // parts).reshape((-1,) + (1,) * (len(dims) - 1 - position))
    return loudness


def length_profile(amount, total, bound, lean):
    weights = [(1 << 20) // math.isqrt(rank ** lean) + 1 for rank in range(2, amount + 1)]
    rest, counts = total - bound - (amount - 1), [1] * (amount - 1)
    while rest > 0:
        free = [i for i in range(amount - 1) if counts[i] < bound]
        whole, budget = sum([weights[i] for i in free]), rest
        for i in free:
            extra = min(bound - counts[i], max(1, budget * weights[i] // whole), rest)
            counts[i] = counts[i] + extra
            rest = rest - extra
    return np.array([bound] + counts)


def uneven(key, amount, total, limit, lean):
    if amount == 2:
        one = jax.random.randint(key, (), max(1, total - limit), min(limit, total - 1) + 1)
        return jnp.stack([one, total - one])
    sizes = jnp.asarray(length_profile(amount, total, limit, lean), jnp.int32)
    twos = (amount - 1) // 2
    source_of, taker = sizes[1:1 + 2 * twos:2], sizes[2:2 + 2 * twos:2]
    slack = jnp.minimum(source_of - 1, limit - taker)
    shifted = jax.random.randint(jax.random.fold_in(key, 1), (twos,), 0, 1 << 20) % (slack + 1)
    sizes = sizes.at[1:1 + 2 * twos:2].set(source_of - shifted).at[2:2 + 2 * twos:2].set(taker + shifted)
    return sizes[jax.random.permutation(jax.random.fold_in(key, 2), amount)]


def noise(key, shape, spread, reach, split=(), held_as=jnp.bfloat16):
    drawn = spread * jax.random.normal(key, shape, jnp.float32)
    if split:
        drawn = drawn * block_scale(key, shape, split, -0.22, 0.18)
    return jnp.clip(drawn, -reach, reach).astype(held_as)


def setup_inputs(seed: int = 0) -> dict:
    seeds = jax.random.split(jax.random.key(seed), 8)
    object_field = noise(seeds[0], (2, NH, NW), 0.5, 3.0, ((1, 48), (2, 16)), jnp.float32)
    probe_field = noise(seeds[1], (2, PW, PW), 1.0, 6.0, (), jnp.float32)
    amplitudes = jnp.clip(jnp.exp(math.log(16.0) - 3.465736 * jax.random.uniform(seeds[2], (N_ROW, N_COL, POOL, PW, PW), jnp.float32) ** block_scale(seeds[2], (N_ROW, N_COL, POOL, PW, PW), ((0, 48), (1, 16)), -0.2, 0.2)), 0.5, 16.0).astype(jnp.bfloat16)
    pos_rows = touch_ends(jax.random.randint(seeds[3], (N_ROW, N_COL, POOL), 0, TH), jax.random.fold_in(seeds[3], 1), 0, TH - 1).astype(jnp.int32)
    pos_cols = touch_ends(jax.random.randint(seeds[4], (N_ROW, N_COL, POOL), 0, TW), jax.random.fold_in(seeds[4], 1), 0, TW - 1).astype(jnp.int32)
    scan_pick = touch_ends(jax.random.randint(seeds[5], (N_ROW, N_COL, SCAP), 0, POOL), jax.random.fold_in(seeds[5], 1), 0, POOL - 1).astype(jnp.int32)
    scan_count = uneven(seeds[6], TILES, USED, SCAP, 2).astype(jnp.int32)
    return dict(object_field=object_field, probe_field=probe_field, amplitudes=amplitudes, pos_rows=pos_rows, pos_cols=pos_cols, scan_pick=scan_pick, scan_count=scan_count)


PRECISE = lax.Precision.HIGHEST
SOFTENING = 0.25
OBJECT_REG = 0.5
PROBE_REG = 1.0

def dft_tables(patch_width):
    grid_index = jnp.arange(patch_width, dtype=jnp.int32)
    phase_angle = (grid_index[:, None] * grid_index[None, :] % patch_width).astype(jnp.float32) * (2.0 * math.pi / patch_width)
    factor = 1.0 / math.sqrt(patch_width)
    return (jnp.cos(phase_angle) * factor, -jnp.sin(phase_angle) * factor)

def left_apply(table, data):
    return jnp.einsum('ka,sab->skb', table, data, precision=PRECISE)

def right_apply(data, table):
    return jnp.einsum('sab,bk->sak', data, table, precision=PRECISE)

def transform(real_part, imag_part, table_re, table_im):
    left_re = left_apply(table_re, real_part) - left_apply(table_im, imag_part)
    left_im = left_apply(table_re, imag_part) + left_apply(table_im, real_part)
    out_re = right_apply(left_re, table_re) - right_apply(left_im, table_im)
    out_im = right_apply(left_re, table_im) + right_apply(left_im, table_re)
    return (out_re, out_im)

def tile_terms(extended, probe_field, amps_tile, row_at, col_at, picks, count):
    patch_width = probe_field.shape[1]
    slot_count = picks.shape[0]
    table_re, table_im = dft_tables(patch_width)
    measured = amps_tile[picks].astype(jnp.float32)
    row_pick = row_at[picks].astype(jnp.int32)
    col_pick = col_at[picks].astype(jnp.int32)
    slot_live = (jnp.arange(slot_count, dtype=jnp.int32) < count).astype(jnp.float32)
    zero_idx = jnp.zeros((), jnp.int32)

    def cut_patch(row_start, col_start):
        return lax.dynamic_slice(extended, (zero_idx, row_start, col_start), (2, patch_width, patch_width))
    patches = jax.vmap(cut_patch)(row_pick, col_pick)
    object_re = patches[:, 0]
    object_im = patches[:, 1]
    probe_re = probe_field[0]
    probe_im = probe_field[1]
    wave_re = probe_re * object_re - probe_im * object_im
    wave_im = probe_re * object_im + probe_im * object_re
    far_re, far_im = transform(wave_re, wave_im, table_re, table_im)
    modulus = jnp.sqrt(far_re * far_re + far_im * far_im + SOFTENING)
    weight = (measured / modulus - 1.0) * slot_live[:, None, None]
    back_re, back_im = transform(far_re * weight, far_im * weight, table_re, -table_im)
    grad_re = probe_re * back_re + probe_im * back_im
    grad_im = probe_re * back_im - probe_im * back_re
    probe_grad_re = lax.optimization_barrier(jnp.sum(object_re * back_re + object_im * back_im, axis=0))
    probe_grad_im = lax.optimization_barrier(jnp.sum(object_re * back_im - object_im * back_re, axis=0))
    probe_light = lax.optimization_barrier(jnp.sum(slot_live[:, None, None] * (object_re * object_re + object_im * object_im), axis=0))
    lamp_power = probe_re * probe_re + probe_im * probe_im
    pieces = jnp.stack([grad_re, grad_im, slot_live[:, None, None] * lamp_power[None]], axis=1)
    grad_ext = jnp.zeros((3,) + extended.shape[1:], jnp.float32)

    def place_patch(slot_idx, running_sum):
        corner_at = (zero_idx, row_pick[slot_idx], col_pick[slot_idx])
        current = lax.dynamic_slice(running_sum, corner_at, (3, patch_width, patch_width))
        return lax.dynamic_update_slice(running_sum, current + pieces[slot_idx], corner_at)
    grad_ext = lax.fori_loop(0, slot_count, place_patch, grad_ext)
    return (grad_ext, (probe_grad_re, probe_grad_im, probe_light))

def reference(object_field, probe_field, amplitudes, pos_rows, pos_cols, scan_pick, scan_count):
    rim_width = PW // 2
    padded = jnp.pad(object_field, ((0, 0), (rim_width, rim_width), (rim_width, rim_width)))
    grad_all = jnp.zeros((3, NH + 2 * rim_width, NW + 2 * rim_width), jnp.float32)
    zero_plane = jnp.zeros((PW, PW), jnp.float32)
    zero_idx = jnp.zeros((), jnp.int32)

    def per_tile(tile_idx, carry):
        grad_now, sums_now = carry
        tile_pos = jnp.asarray(tile_idx).astype(jnp.int32)
        tile_row = tile_pos // N_COL
        tile_col = tile_pos % N_COL
        corner_at = (zero_idx, (tile_row * TH).astype(jnp.int32), (tile_col * TW).astype(jnp.int32))
        extended = lax.dynamic_slice(padded, corner_at, (2, TH + 2 * rim_width, TW + 2 * rim_width))
        grad_ext, probe_terms = tile_terms(extended, probe_field, amplitudes[tile_row, tile_col], pos_rows[tile_row, tile_col], pos_cols[tile_row, tile_col], scan_pick[tile_row, tile_col], scan_count[tile_pos])
        current = lax.dynamic_slice(grad_now, corner_at, (3, TH + 2 * rim_width, TW + 2 * rim_width))
        grad_now = lax.dynamic_update_slice(grad_now, current + grad_ext, corner_at)
        sums_now = (sums_now[0] + probe_terms[0], sums_now[1] + probe_terms[1], sums_now[2] + probe_terms[2])
        return (grad_now, sums_now)
    grad_all, probe_sums = lax.fori_loop(0, N_ROW * N_COL, per_tile, (grad_all, (zero_plane, zero_plane, zero_plane)))
    inside = grad_all[:, rim_width:rim_width + NH, rim_width:rim_width + NW]
    object_next = object_field + inside[0:2] / (inside[2] + OBJECT_REG)
    probe_next = probe_field + jnp.stack([probe_sums[0], probe_sums[1]]) / (probe_sums[2] + PROBE_REG)
    return (object_next, probe_next)
```

```python
import math

import jax
import jax.numpy as jnp
import numpy as np
from jax import lax
from jax.experimental import pallas as pl
from jax.experimental.pallas import tpu as pltpu
from jax.sharding import Mesh
from jax.sharding import PartitionSpec as P

SOFTENING = 0.25
OBJECT_REG = 0.5
PROBE_REG = 1.0
F32, BF16 = jnp.float32, jnp.bfloat16
VMEM_LIMIT = 60 * 1024 * 1024


def half_tables(width):
    half = width // 2
    n = np.arange(half)
    tables = []
    for odd in (0, 1):
        turn = ((2 * n[:, None] + odd) * n[None, :]) % width * (2.0 * np.pi / width)
        c, s = np.cos(turn) / math.sqrt(width), np.sin(turn) / math.sqrt(width)
        tables.append(np.block([[c, s], [-s, c]]))
    tables += [tables[0].T, tables[1].T]
    full = jnp.asarray(np.stack(tables), F32)
    high = full.astype(BF16)
    low = (full - high.astype(F32)).astype(BF16)
    return high, low


def sorting_table(width):
    order = np.concatenate([np.arange(0, width, 2), np.arange(1, width, 2)])
    return jnp.asarray(np.eye(width, dtype=np.float32)[order], BF16)


def dot(a, b):
    return lax.dot_general(a, b, (((1,), (0,)), ((), ())), preferred_element_type=F32)


def halves(x):
    high = x.astype(BF16)
    return high, (x - high.astype(F32)).astype(BF16)


def data_by_table(data, high, low):
    dh, dl = halves(data)
    return dot(dh, high) + (dot(dl, high) + dot(dh, low))


def table_by_data(high, low, data):
    dh, dl = halves(data)
    return dot(high, dh) + (dot(high, dl) + dot(low, dh))


def amplitude_kernel(pick, amps, order, out):
    ordered_rows = dot(order[...], amps[0]).astype(BF16)
    out[0] = lax.dot_general(
        ordered_rows, order[...], (((1,), (1,)), ((), ())), preferred_element_type=F32
    ).astype(BF16)


def ordered_amplitudes(amps, picks):
    slots, width = picks.shape[0], amps.shape[-1]
    return pl.pallas_call(
        amplitude_kernel,
        grid_spec=pltpu.PrefetchScalarGridSpec(
            num_scalar_prefetch=1,
            grid=(slots,),
            in_specs=[
                pl.BlockSpec((1, width, width), lambda s, pick: (pick[s], 0, 0)),
                pl.BlockSpec((width, width), lambda s, pick: (0, 0)),
            ],
            out_specs=pl.BlockSpec((1, width, width), lambda s, pick: (s, 0, 0)),
        ),
        out_shape=jax.ShapeDtypeStruct((slots, width, width), BF16),
        name="amplitude_order",
    )(picks, amps, sorting_table(width))


def scan_kernel(
    pick, rows_at, cols_at, count,
    center, above, below, left, right, probe, amps, high, low,
    grad_left, grad_center, grad_right, sums,
    ext, grad,
):
    width = probe.shape[1]
    rim = width // 2
    tall, wide = ext.shape[1:]
    th, tw = center.shape[1:]
    slots = amps.shape[0]
    ext[:, 0:rim, rim : rim + tw] = above[...]
    ext[:, rim : rim + th, rim : rim + tw] = center[...]
    ext[:, rim + th :, rim : rim + tw] = below[...]
    ext[:, :, 0:rim] = left[...]
    ext[:, :, rim + tw :] = right[...]
    grad[...] = jnp.zeros_like(grad)
    pr, pi = probe[0], probe[1]
    power = pr * pr + pi * pi
    total = [jnp.zeros((width, width), F32) for _ in range(3)]
    for s in range(slots):
        j = pick[s]
        r, c = rows_at[j], cols_at[j]
        live = (s < count[0]).astype(F32)
        skew = lax.rem(r, 8)
        rows = pl.ds(pl.multiple_of(r - skew, 8), width + 8)
        up = lax.rem(width + 8 - skew, width + 8)
        back = lax.rem(wide - c, wide)

        def cut(plane):
            block = pltpu.roll(ext[plane, rows, :], back, 1)[:, :width]
            return pltpu.roll(block, up, 0)[:width]

        o_r, o_i = cut(0), cut(1)
        w_r, w_i = pr * o_r - pi * o_i, pr * o_i + pi * o_r
        even = jnp.concatenate([w_r[:rim] + w_r[rim:], w_i[:rim] + w_i[rim:]], axis=0)
        odd = jnp.concatenate([w_r[:rim] - w_r[rim:], w_i[:rim] - w_i[rim:]], axis=0)
        even = table_by_data(high[0], low[0], even)
        odd = table_by_data(high[1], low[1], odd)
        y_r = jnp.concatenate([even[:rim], odd[:rim]], axis=0)
        y_i = jnp.concatenate([even[rim:], odd[rim:]], axis=0)
        even = jnp.concatenate([y_r[:, :rim] + y_r[:, rim:], y_i[:, :rim] + y_i[:, rim:]], axis=1)
        odd = jnp.concatenate([y_r[:, :rim] - y_r[:, rim:], y_i[:, :rim] - y_i[:, rim:]], axis=1)
        even = data_by_table(even, high[2], low[2])
        odd = data_by_table(odd, high[3], low[3])
        m = amps[s].astype(F32)

        def weighted(z, m):
            re, im = z[:, :rim], z[:, rim:]
            weight = (m * lax.rsqrt(re * re + im * im + SOFTENING) - 1.0) * live
            return jnp.concatenate([re * weight, im * weight], axis=1)

        even = data_by_table(weighted(even, m[:, :rim]), high[0], low[0])
        odd = data_by_table(weighted(odd, m[:, rim:]), high[1], low[1])
        plus, minus = even + odd, even - odd
        y_r = jnp.concatenate([plus[:, :rim], minus[:, :rim]], axis=1)
        y_i = jnp.concatenate([plus[:, rim:], minus[:, rim:]], axis=1)
        even = table_by_data(high[2], low[2], jnp.concatenate([y_r[:rim], y_i[:rim]], axis=0))
        odd = table_by_data(high[3], low[3], jnp.concatenate([y_r[rim:], y_i[rim:]], axis=0))
        plus, minus = even + odd, even - odd
        d_r = jnp.concatenate([plus[:rim], minus[:rim]], axis=0)
        d_i = jnp.concatenate([plus[rim:], minus[rim:]], axis=0)
        total[0] += o_r * d_r + o_i * d_i
        total[1] += o_r * d_i - o_i * d_r
        total[2] += live * (o_r * o_r + o_i * o_i)
        pieces = (pr * d_r + pi * d_i, pr * d_i - pi * d_r, live * power)
        for plane, piece in enumerate(pieces):
            tail = jnp.zeros((8, width), F32)
            spread = pltpu.roll(jnp.concatenate([piece, tail], axis=0), skew, 0)
            spread = jnp.concatenate([spread, jnp.zeros((width + 8, wide - width), F32)], axis=1)
            grad[plane, rows, :] += pltpu.roll(spread, c, 1)
    parts, _, part = sums.shape[:3]
    for plane in range(3):
        for p in range(parts):
            sums[p, plane] = total[plane][p * part : (p + 1) * part]
    grad_left[...] = grad[:, :, 0:rim]
    grad_center[...] = grad[:, :, rim : rim + tw]
    grad_right[...] = grad[:, :, rim + tw :]


def scans(picks, rows_at, cols_at, count, center, above, below, left, right, probe, amps, parts):
    width = probe.shape[1]
    rim = width // 2
    th, tw = center.shape[1:]
    tall, wide = th + 2 * rim, tw + 2 * rim
    high, low = half_tables(width)
    smem = pl.BlockSpec(memory_space=pltpu.SMEM)
    vmem = pl.BlockSpec(memory_space=pltpu.VMEM)
    return pl.pallas_call(
        scan_kernel,
        in_specs=[smem] * 4 + [vmem] * 9,
        out_specs=[vmem] * 4,
        out_shape=[
            jax.ShapeDtypeStruct((3, tall, rim), F32),
            jax.ShapeDtypeStruct((3, tall, tw), F32),
            jax.ShapeDtypeStruct((3, tall, rim), F32),
            jax.ShapeDtypeStruct((parts, 3, width // parts, width), F32),
        ],
        scratch_shapes=[pltpu.VMEM((2, tall, wide), F32), pltpu.VMEM((3, tall, wide), F32)],
        compiler_params=pltpu.CompilerParams(vmem_limit_bytes=VMEM_LIMIT),
        name="scan_step",
    )(picks, rows_at, cols_at, count, center, above, below, left, right, probe, amps, high, low)


ROW = ("y_lo", "z")
COL = ("y_hi", "x", "core")
NEAR = ("x", "core")
FAR = ("y_lo", "z", "y_hi")
SPLIT = {"y_lo": 4, "z": 12, "y_hi": 2, "x": 4, "core": 2}


def neighbours(last, first, axis):
    peers = lax.axis_size(axis)
    up = [(i, i + 1) for i in range(peers - 1)]
    down = [(j, i) for i, j in up]
    return lax.ppermute(last, axis, up), lax.ppermute(first, axis, down)


def exchanged(array, axes):
    return lax.all_to_all(array, axes, 0, 0, tiled=True)


def to_all(array, axes):
    return exchanged(jnp.broadcast_to(array[None], (lax.axis_size(axes),) + array.shape), axes)


def probe_update(sums, probe_field):
    near, _, part, width = sums.shape
    mine = exchanged(sums, NEAR).sum(0)
    far = lax.axis_size(FAR)
    mine = exchanged(mine.reshape(far, -1, width), FAR).sum(0)
    mine = to_all(mine, FAR).reshape(3, part, width)
    old = lax.dynamic_slice_in_dim(probe_field, lax.axis_index(NEAR) * part, part, axis=1)
    new = to_all(old + mine[0:2] / (mine[2] + PROBE_REG), NEAR)
    return new.transpose(1, 0, 2, 3).reshape(probe_field.shape)


def per_device(object_field, probe_field, amplitudes, pos_rows, pos_cols, scan_pick, scan_count):
    width = probe_field.shape[1]
    rim = width // 2
    th, tw = object_field.shape[1:]
    picks = scan_pick[0, 0]
    above, below = neighbours(object_field[:, th - rim :], object_field[:, :rim], ROW)
    amps = ordered_amplitudes(amplitudes[0, 0], picks)

    def column(part):
        return jnp.concatenate([above[:, :, part], object_field[:, :, part], below[:, :, part]], axis=1)

    left, right = neighbours(column(slice(tw - rim, tw)), column(slice(0, rim)), COL)
    grad_left, grad, grad_right, sums = scans(
        picks, pos_rows[0, 0], pos_cols[0, 0], scan_count,
        object_field, above, below, left, right, probe_field, amps, lax.axis_size(NEAR),
    )
    from_left, from_right = neighbours(grad_right, grad_left, COL)
    grad = jnp.concatenate([grad[:, :, :rim] + from_left, grad[:, :, rim:] + from_right], axis=2)
    from_above, from_below = neighbours(grad[:, th + rim :], grad[:, :rim], ROW)
    grad = grad[:, rim : rim + th]
    grad = grad.at[:, :rim].add(from_above).at[:, th - rim :].add(from_below)
    object_next = object_field + grad[0:2] / (grad[2] + OBJECT_REG)
    return object_next, probe_update(sums, probe_field)


def solution(mesh):
    fine = Mesh(mesh.devices.reshape(tuple(SPLIT.values())), tuple(SPLIT))
    in_specs = (
        P(None, ROW, COL),
        P(),
        P(ROW, COL, None, None, None),
        P(ROW, COL, None),
        P(ROW, COL, None),
        P(ROW, COL, None),
        P(ROW + COL),
    )
    out_specs = (P(None, ROW, COL), P())
    return jax.shard_map(per_device, mesh=fine, in_specs=in_specs, out_specs=out_specs, check_vma=False)
```

```python
import math

import jax
import jax.numpy as jnp
import numpy as np
from jax import lax
from jax.experimental import pallas as pl
from jax.experimental.pallas import tpu as pltpu
from jax.sharding import Mesh
from jax.sharding import PartitionSpec as P


SOFTENING = 0.25
OBJECT_REG = 0.5
PROBE_REG = 1.0
F32, BF16 = jnp.float32, jnp.bfloat16
VMEM_LIMIT = 24 * 1024 * 1024
SMALL_VMEM = 10 * 1024 * 1024
NOTE = 11
TAIL = 8


def half_tables(width):
    half = width // 2
    n = np.arange(half)
    tables = []
    for odd in (0, 1):
        turn = ((2 * n[:, None] + odd) * n[None, :]) % width * (2.0 * np.pi / width)
        c, s = np.cos(turn) / math.sqrt(width), np.sin(turn) / math.sqrt(width)
        tables.append(np.block([[c, s], [-s, c]]))
    tables += [tables[0].T, tables[1].T]
    full = jnp.asarray(np.stack(tables), F32)
    high = full.astype(BF16)
    low = (full - high.astype(F32)).astype(BF16)
    return high, low


def sorting_table(width):
    order = np.concatenate([np.arange(0, width, 2), np.arange(1, width, 2)])
    return jnp.asarray(np.eye(width, dtype=np.float32)[order], BF16)


def dot(a, b):
    return lax.dot_general(a, b, (((1,), (0,)), ((), ())), preferred_element_type=F32)


def halves(x):
    high = x.astype(BF16)
    return high, (x - high.astype(F32)).astype(BF16)


def data_by_table(data, high, low):
    dh, dl = halves(data)
    return dot(dh, high) + (dot(dl, high) + dot(dh, low))


def table_by_data(high, low, data):
    dh, dl = halves(data)
    return dot(high, dh) + (dot(high, dl) + dot(low, dh))


def amplitude_kernel(pick, amps, order, out):
    ordered_rows = dot(order[...], amps[0]).astype(BF16)
    out[0] = lax.dot_general(
        ordered_rows, order[...], (((1,), (1,)), ((), ())), preferred_element_type=F32
    ).astype(BF16)


def ordered_amplitudes(amps, picks):
    slots, width = picks.shape[0], amps.shape[-1]
    return pl.pallas_call(
        amplitude_kernel,
        grid_spec=pltpu.PrefetchScalarGridSpec(
            num_scalar_prefetch=1,
            grid=(slots,),
            in_specs=[
                pl.BlockSpec((1, width, width), lambda s, pick: (pick[s], 0, 0)),
                pl.BlockSpec((width, width), lambda s, pick: (0, 0)),
            ],
            out_specs=pl.BlockSpec((1, width, width), lambda s, pick: (s, 0, 0)),
        ),
        out_shape=jax.ShapeDtypeStruct((slots, width, width), BF16),
        compiler_params=pltpu.CompilerParams(vmem_limit_bytes=SMALL_VMEM),
        name="amplitude_order",
    )(picks, amps, sorting_table(width))


def scan_kernel(
    pick, rows_at, cols_at, count,
    center, above, below, left, right, corners_above, corners_below, probe, amps, high, low,
    grad_above, grad_center, grad_below, sums,
    ext, grad,
):
    width = probe.shape[1]
    rim = width // 2
    _, wide = ext.shape[1:]
    th, tw = center.shape[1:]
    slots = amps.shape[0]
    ext[:, rim : rim + th, rim : rim + tw] = center[...]
    for at, side, corners, skip in ((0, above, corners_above, 0), (rim + th, below, corners_below, TAIL)):
        ext[:, at : at + rim, 0:rim] = corners[0:2, skip : skip + rim]
        ext[:, at : at + rim, rim : rim + tw] = side[:, :rim]
        ext[:, at : at + rim, rim + tw :] = corners[2:4, skip : skip + rim]
    ext[:, rim : rim + th, 0:rim] = left[:, TAIL : TAIL + th]
    ext[:, rim : rim + th, rim + tw :] = right[:, TAIL : TAIL + th]
    grad[...] = jnp.zeros_like(grad)
    pr, pi = probe[0], probe[1]
    total = [jnp.zeros((width, width), F32) for _ in range(3)]
    for s in range(slots):
        j = pick[s]
        r, c = rows_at[j], cols_at[j]
        live = (s < count[0]).astype(F32)
        skew = lax.rem(r, 8)
        rows = pl.ds(pl.multiple_of(r - skew, 8), width + 8)
        up = lax.rem(width + 8 - skew, width + 8)
        back = lax.rem(wide - c, wide)

        def cut(plane):
            block = pltpu.roll(ext[plane, rows, :], back, 1)[:, :width]
            return pltpu.roll(block, up, 0)[:width]

        o_r, o_i = cut(0), cut(1)
        w_r, w_i = pr * o_r - pi * o_i, pr * o_i + pi * o_r
        even = jnp.concatenate([w_r[:rim] + w_r[rim:], w_i[:rim] + w_i[rim:]], axis=0)
        odd = jnp.concatenate([w_r[:rim] - w_r[rim:], w_i[:rim] - w_i[rim:]], axis=0)
        even = table_by_data(high[0], low[0], even)
        odd = table_by_data(high[1], low[1], odd)
        y_r = jnp.concatenate([even[:rim], odd[:rim]], axis=0)
        y_i = jnp.concatenate([even[rim:], odd[rim:]], axis=0)
        even = jnp.concatenate([y_r[:, :rim] + y_r[:, rim:], y_i[:, :rim] + y_i[:, rim:]], axis=1)
        odd = jnp.concatenate([y_r[:, :rim] - y_r[:, rim:], y_i[:, :rim] - y_i[:, rim:]], axis=1)
        even = data_by_table(even, high[2], low[2])
        odd = data_by_table(odd, high[3], low[3])
        m = amps[s].astype(F32)

        def weighted(z, m):
            re, im = z[:, :rim], z[:, rim:]
            weight = (m * lax.rsqrt(re * re + im * im + SOFTENING) - 1.0) * live
            return jnp.concatenate([re * weight, im * weight], axis=1)

        even = data_by_table(weighted(even, m[:, :rim]), high[0], low[0])
        odd = data_by_table(weighted(odd, m[:, rim:]), high[1], low[1])
        plus, minus = even + odd, even - odd
        y_r = jnp.concatenate([plus[:, :rim], minus[:, :rim]], axis=1)
        y_i = jnp.concatenate([plus[:, rim:], minus[:, rim:]], axis=1)
        even = table_by_data(high[2], low[2], jnp.concatenate([y_r[:rim], y_i[:rim]], axis=0))
        odd = table_by_data(high[3], low[3], jnp.concatenate([y_r[rim:], y_i[rim:]], axis=0))
        plus, minus = even + odd, even - odd
        d_r = jnp.concatenate([plus[:rim], minus[:rim]], axis=0)
        d_i = jnp.concatenate([plus[rim:], minus[rim:]], axis=0)
        total[0] += o_r * d_r + o_i * d_i
        total[1] += o_r * d_i - o_i * d_r
        total[2] += live * (o_r * o_r + o_i * o_i)
        pieces = (pr * d_r + pi * d_i, pr * d_i - pi * d_r)
        for plane, piece in enumerate(pieces):
            tail = jnp.zeros((8, width), F32)
            spread = pltpu.roll(jnp.concatenate([piece, tail], axis=0), skew, 0)
            spread = jnp.concatenate([spread, jnp.zeros((width + 8, wide - width), F32)], axis=1)
            grad[plane, rows, :] += pltpu.roll(spread, c, 1)
    parts = sums.shape[0]
    part = width // parts
    for p in range(parts):
        for q in range(6):
            lanes = slice((q % 2) * rim, (q % 2 + 1) * rim)
            sums[p, q * part : (q + 1) * part] = total[q // 2][p * part : (p + 1) * part, lanes]
    grad_above[...] = grad[:, 0:rim]
    grad_center[...] = grad[:, rim : rim + th]
    grad_below[...] = grad[:, rim + th :]


def scans(picks, rows_at, cols_at, count, center, edges, probe, amps, parts):
    width = probe.shape[1]
    rim = width // 2
    th, tw = center.shape[1:]
    tall, wide = th + 2 * rim, tw + 2 * rim
    high, low = half_tables(width)
    smem = pl.BlockSpec(memory_space=pltpu.SMEM)
    vmem = pl.BlockSpec(memory_space=pltpu.VMEM)
    return pl.pallas_call(
        scan_kernel,
        in_specs=[smem] * 4 + [vmem] * 11,
        out_specs=[vmem] * 4,
        out_shape=[
            jax.ShapeDtypeStruct((2, rim, wide), F32),
            jax.ShapeDtypeStruct((2, th, wide), F32),
            jax.ShapeDtypeStruct((2, rim, wide), F32),
            jax.ShapeDtypeStruct((parts, 6 * width // parts, rim), F32),
        ],
        scratch_shapes=[pltpu.VMEM((2, tall, wide), F32), pltpu.VMEM((2, tall, wide), F32)],
        compiler_params=pltpu.CompilerParams(vmem_limit_bytes=VMEM_LIMIT),
        name="scan_step",
    )(picks, rows_at, cols_at, count, center, *edges, probe, amps, high, low)


def piece_kernel(index, sums, probe, out):
    parts, rows, half = out.shape
    part = rows // 4
    at = pl.multiple_of(index[0] * part, part)
    for q in range(4):
        old = probe[q // 2, pl.ds(at, part), (q % 2) * half : (q % 2 + 1) * half]
        grad, light = sums[q * part : (q + 1) * part], sums[(4 + q % 2) * part : (5 + q % 2) * part]
        new = old + grad / (light + PROBE_REG)
        for p in range(parts):
            out[p, q * part : (q + 1) * part] = new


def probe_piece(sums, probe, parts, index):
    half = probe.shape[2] // 2
    vmem = pl.BlockSpec(memory_space=pltpu.VMEM)
    return pl.pallas_call(
        piece_kernel,
        in_specs=[pl.BlockSpec(memory_space=pltpu.SMEM), vmem, vmem],
        out_specs=vmem,
        out_shape=jax.ShapeDtypeStruct((parts, 4 * probe.shape[1] // parts, half), F32),
        compiler_params=pltpu.CompilerParams(vmem_limit_bytes=SMALL_VMEM),
        name="probe_piece",
    )(index.astype(jnp.int32).reshape(1), sums, probe)


def join_kernel(pieces, out):
    parts, rows, half = pieces.shape
    part = rows // 4
    for p in range(parts):
        for q in range(4):
            lanes = slice((q % 2) * half, (q % 2 + 1) * half)
            out[q // 2, p * part : (p + 1) * part, lanes] = pieces[p, q * part : (q + 1) * part]


def probe_joined(pieces, probe):
    vmem = pl.BlockSpec(memory_space=pltpu.VMEM)
    return pl.pallas_call(
        join_kernel,
        in_specs=[vmem],
        out_specs=vmem,
        out_shape=jax.ShapeDtypeStruct(probe.shape, F32),
        compiler_params=pltpu.CompilerParams(vmem_limit_bytes=SMALL_VMEM),
        name="probe_join",
    )(pieces)


def light_kernel(scans_at, probe, share, lit):
    width = probe.shape[1]
    rim = width // 2
    th, tw = share.shape
    wide = tw + 2 * rim
    lit[...] = jnp.zeros_like(lit)
    power = probe[0] * probe[0] + probe[1] * probe[1]
    power = jnp.concatenate([power, jnp.zeros((8, width), F32)], axis=0)
    power = jnp.concatenate([power, jnp.zeros((width + 8, wide - width), F32)], axis=1)
    for down in range(3):
        for right in range(3):
            for s in range(2):
                base = NOTE * (3 * down + right)

                @pl.when(s < scans_at[base + 10])
                def _():
                    j = base + scans_at[base + 8 + s]
                    r, c = scans_at[j], scans_at[j + 4]
                    skew = lax.rem(r, 8)
                    rows = pl.ds(pl.multiple_of(r - skew + down * th, 8), width + 8)
                    placed = pltpu.roll(pltpu.roll(power, skew, 0), c, 1)
                    lit[rows, right * tw : right * tw + wide] += placed

    share[...] = 1.0 / (lit[th + rim : 2 * th + rim, tw + rim : 2 * tw + rim] + OBJECT_REG)


def light_share(scans_at, probe, th, tw):
    width = probe.shape[1]
    rim = width // 2
    return pl.pallas_call(
        light_kernel,
        in_specs=[pl.BlockSpec(memory_space=pltpu.SMEM), pl.BlockSpec(memory_space=pltpu.VMEM)],
        out_specs=pl.BlockSpec(memory_space=pltpu.VMEM),
        out_shape=jax.ShapeDtypeStruct((th, tw), F32),
        scratch_shapes=[pltpu.VMEM((3 * th + 2 * rim, 3 * tw + 2 * rim), F32)],
        compiler_params=pltpu.CompilerParams(vmem_limit_bytes=SMALL_VMEM),
        cost_estimate=pl.CostEstimate(flops=20_000_000, bytes_accessed=1_000_000, transcendentals=0),
        name="light_share",
    )(scans_at, probe)


ROW = ("y_lo", "z_hi", "z_lo")
COL = ("y_hi", "x", "core")
NEAR = ("x", "core")
MID = ("y_lo", "y_hi")
SPLIT = {"y_lo": 4, "z_hi": 3, "z_lo": 4, "y_hi": 2, "x": 4, "core": 2}


def neighbours(last, first, axis):
    peers = lax.axis_size(axis)
    up = [(i, i + 1) for i in range(peers - 1)]
    down = [(j, i) for i, j in up]
    return lax.ppermute(last, axis, up), lax.ppermute(first, axis, down)


def exchanged(array, axes):
    return lax.all_to_all(array.reshape(lax.axis_size(axes), -1, array.shape[-1]), axes, 0, 0, tiled=True)


def copied(array, axes):
    return jnp.broadcast_to(array[None], (lax.axis_size(axes),) + array.shape)


def halo(object_field, note):
    rim = note.shape[0]
    th, tw = object_field.shape[1:]
    tail = jnp.broadcast_to(note, (2, TAIL, rim))
    tail_wide = jnp.concatenate([tail] * (tw // rim), axis=2)

    def column(part):
        return jnp.concatenate([tail, object_field[:, :, part], tail], axis=1)

    def line(part):
        return jnp.concatenate([object_field[:, part], tail_wide], axis=1)

    def corner(part):
        return jnp.concatenate([left[:, part], right[:, part]], axis=0)

    left, right = neighbours(column(slice(tw - rim, tw)), column(slice(0, rim)), COL)
    above, below = neighbours(line(slice(th - rim, th)), line(slice(0, rim)), ROW)
    corners_above, corners_below = neighbours(
        corner(slice(TAIL + th - rim, TAIL + th + TAIL)), corner(slice(0, TAIL + rim)), ROW
    )
    notes = [
        corners_above[0, rim, :NOTE], above[0, rim, :NOTE], corners_above[2, rim, :NOTE],
        left[0, 0, :NOTE], note[:NOTE], right[0, 0, :NOTE],
        corners_below[0, 0, :NOTE], below[0, rim, :NOTE], corners_below[2, 0, :NOTE],
    ]
    edges = (above, below, left, right, corners_above, corners_below)
    return edges, jnp.concatenate(notes).astype(jnp.int32)


def folded(grad, above, below):
    rim = above.shape[1]
    th = grad.shape[1]
    from_above, from_below = neighbours(below, above, ROW)
    grad = jnp.concatenate(
        [grad[:, :rim] + from_above, grad[:, rim : th - rim], grad[:, th - rim :] + from_below], axis=1
    )
    from_left, from_right = neighbours(grad[:, :, -rim:], grad[:, :, :rim], COL)
    grad = grad[:, :, rim:-rim]
    return jnp.concatenate([grad[:, :, :rim] + from_left, grad[:, :, rim:] + from_right], axis=2)


def per_device(object_field, probe_field, amplitudes, pos_rows, pos_cols, scan_pick, scan_count):
    width = probe_field.shape[1]
    rim = width // 2
    th, tw = object_field.shape[1:]
    picks, rows_at, cols_at = scan_pick[0, 0], pos_rows[0, 0], pos_cols[0, 0]
    near = lax.axis_size(NEAR)
    own = jnp.concatenate([rows_at, cols_at, picks, scan_count])
    edges, scans_at = halo(object_field, jnp.pad(own.astype(F32), (0, rim - NOTE)))
    amps = ordered_amplitudes(amplitudes[0, 0], picks)
    above, grad, below, sums = scans(
        picks, rows_at, cols_at, scan_count, object_field, edges, probe_field, amps, near
    )
    share = light_share(scans_at, probe_field, th, tw)
    mine = exchanged(sums, NEAR).sum(0)
    above, below, mine = lax.optimization_barrier((above, below, mine))
    mine = exchanged(mine, MID)
    share, mine = lax.optimization_barrier((share, mine))
    grad = folded(grad, above, below)
    mine = mine.sum(0)
    mine = exchanged(copied(mine, ("z_lo",)), ("z_lo",)).sum(0)
    mine = exchanged(copied(mine, ("z_hi",)), ("z_hi",)).sum(0)
    mine = exchanged(copied(mine, MID), MID).reshape(-1, rim)
    mine = exchanged(probe_piece(mine, probe_field, near, lax.axis_index(NEAR)), NEAR)
    return object_field + grad * share, probe_joined(mine, probe_field)


def solution(mesh):
    fine = Mesh(mesh.devices.reshape(tuple(SPLIT.values())), tuple(SPLIT))
    in_specs = (
        P(None, ROW, COL),
        P(),
        P(ROW, COL, None, None, None),
        P(ROW, COL, None),
        P(ROW, COL, None),
        P(ROW, COL, None),
        P(ROW + COL),
    )
    out_specs = (P(None, ROW, COL), P())

    return jax.shard_map(per_device, mesh=fine, in_specs=in_specs, out_specs=out_specs, check_vma=False)
```

```python
import math

import jax
import jax.numpy as jnp
import numpy as np
from jax import lax
from jax.experimental import pallas as pl
from jax.experimental.pallas import tpu as pltpu
from jax.sharding import Mesh
from jax.sharding import PartitionSpec as P


SOFTENING = 0.25
OBJECT_REG = 0.5
PROBE_REG = 1.0
F32, BF16 = jnp.float32, jnp.bfloat16
VMEM_LIMIT = 24 * 1024 * 1024
SMALL_VMEM = 10 * 1024 * 1024
NOTE = 11
TAIL = 8


def half_tables(width):
    half = width // 2
    n = np.arange(half)
    tables = []
    for odd in (0, 1):
        turn = ((2 * n[:, None] + odd) * n[None, :]) % width * (2.0 * np.pi / width)
        c, s = np.cos(turn) / math.sqrt(width), np.sin(turn) / math.sqrt(width)
        tables.append(np.block([[c, s], [-s, c]]))
    tables += [tables[0].T, tables[1].T]
    full = jnp.asarray(np.stack(tables), F32)
    high = full.astype(BF16)
    low = (full - high.astype(F32)).astype(BF16)
    return high, low


def sorting_table(width):
    order = np.concatenate([np.arange(0, width, 2), np.arange(1, width, 2)])
    return jnp.asarray(np.eye(width, dtype=np.float32)[order], BF16)


def dot(a, b):
    return lax.dot_general(a, b, (((1,), (0,)), ((), ())), preferred_element_type=F32)


def halves(x):
    high = x.astype(BF16)
    return high, (x - high.astype(F32)).astype(BF16)


def data_by_table(data, high, low):
    dh, dl = halves(data)
    return dot(dh, high) + (dot(dl, high) + dot(dh, low))


def table_by_data(high, low, data):
    dh, dl = halves(data)
    return dot(high, dh) + (dot(high, dl) + dot(low, dh))


def amplitude_kernel(pick, amps, order, out):
    ordered_rows = dot(order[...], amps[0]).astype(BF16)
    out[0] = lax.dot_general(
        ordered_rows, order[...], (((1,), (1,)), ((), ())), preferred_element_type=F32
    ).astype(BF16)


def ordered_amplitudes(amps, picks):
    slots, width = picks.shape[0], amps.shape[-1]
    return pl.pallas_call(
        amplitude_kernel,
        grid_spec=pltpu.PrefetchScalarGridSpec(
            num_scalar_prefetch=1,
            grid=(slots,),
            in_specs=[
                pl.BlockSpec((1, width, width), lambda s, pick: (pick[s], 0, 0)),
                pl.BlockSpec((width, width), lambda s, pick: (0, 0)),
            ],
            out_specs=pl.BlockSpec((1, width, width), lambda s, pick: (s, 0, 0)),
        ),
        out_shape=jax.ShapeDtypeStruct((slots, width, width), BF16),
        compiler_params=pltpu.CompilerParams(vmem_limit_bytes=SMALL_VMEM),
        name="amplitude_order",
    )(picks, amps, sorting_table(width))


def scan_kernel(
    pick, rows_at, cols_at, count, odd,
    center, col_a, col_b, row_a, row_b, probe, amps, high, low,
    grad_a, grad_center, grad_b, sums,
    ext, grad,
):
    width = probe.shape[1]
    rim = width // 2
    _, wide = ext.shape[1:]
    th, tw = center.shape[1:]
    slots = amps.shape[0]
    foot, side = rim + th, rim + tw
    lines = [pl.ds(pl.multiple_of(at, rim), rim) for at in (foot * (1 - odd[0]), foot * odd[0])]
    lanes = [pl.ds(pl.multiple_of(at, rim), rim) for at in (side * (1 - odd[1]), side * odd[1])]
    ext[:, rim:foot, rim:side] = center[...]
    for line, row in zip(lines, (row_a, row_b)):
        ext[:, line, rim:side] = row[:, :rim, rim:side]
        ext[:, line, lanes[0]] = row[:, :rim, :rim]
        ext[:, line, lanes[1]] = row[:, :rim, side:]
    ext[:, rim:foot, lanes[0]] = col_a[:, :th]
    ext[:, rim:foot, lanes[1]] = col_b[:, :th]
    grad[...] = jnp.zeros_like(grad)
    pr, pi = probe[0], probe[1]
    total = [jnp.zeros((width, width), F32) for _ in range(3)]
    for s in range(slots):
        j = pick[s]
        r, c = rows_at[j], cols_at[j]
        live = (s < count[0]).astype(F32)
        skew = lax.rem(r, 8)
        rows = pl.ds(pl.multiple_of(r - skew, 8), width + 8)
        up = lax.rem(width + 8 - skew, width + 8)
        back = lax.rem(wide - c, wide)

        def cut(plane):
            block = pltpu.roll(ext[plane, rows, :], back, 1)[:, :width]
            return pltpu.roll(block, up, 0)[:width]

        o_r, o_i = cut(0), cut(1)
        w_r, w_i = pr * o_r - pi * o_i, pr * o_i + pi * o_r
        even = jnp.concatenate([w_r[:rim] + w_r[rim:], w_i[:rim] + w_i[rim:]], axis=0)
        odd = jnp.concatenate([w_r[:rim] - w_r[rim:], w_i[:rim] - w_i[rim:]], axis=0)
        even = table_by_data(high[0], low[0], even)
        odd = table_by_data(high[1], low[1], odd)
        y_r = jnp.concatenate([even[:rim], odd[:rim]], axis=0)
        y_i = jnp.concatenate([even[rim:], odd[rim:]], axis=0)
        even = jnp.concatenate([y_r[:, :rim] + y_r[:, rim:], y_i[:, :rim] + y_i[:, rim:]], axis=1)
        odd = jnp.concatenate([y_r[:, :rim] - y_r[:, rim:], y_i[:, :rim] - y_i[:, rim:]], axis=1)
        even = data_by_table(even, high[2], low[2])
        odd = data_by_table(odd, high[3], low[3])
        m = amps[s].astype(F32)

        def weighted(z, m):
            re, im = z[:, :rim], z[:, rim:]
            weight = (m * lax.rsqrt(re * re + im * im + SOFTENING) - 1.0) * live
            return jnp.concatenate([re * weight, im * weight], axis=1)

        even = data_by_table(weighted(even, m[:, :rim]), high[0], low[0])
        odd = data_by_table(weighted(odd, m[:, rim:]), high[1], low[1])
        plus, minus = even + odd, even - odd
        y_r = jnp.concatenate([plus[:, :rim], minus[:, :rim]], axis=1)
        y_i = jnp.concatenate([plus[:, rim:], minus[:, rim:]], axis=1)
        even = table_by_data(high[2], low[2], jnp.concatenate([y_r[:rim], y_i[:rim]], axis=0))
        odd = table_by_data(high[3], low[3], jnp.concatenate([y_r[rim:], y_i[rim:]], axis=0))
        plus, minus = even + odd, even - odd
        d_r = jnp.concatenate([plus[:rim], minus[:rim]], axis=0)
        d_i = jnp.concatenate([plus[rim:], minus[rim:]], axis=0)
        total[0] += o_r * d_r + o_i * d_i
        total[1] += o_r * d_i - o_i * d_r
        total[2] += live * (o_r * o_r + o_i * o_i)
        pieces = (pr * d_r + pi * d_i, pr * d_i - pi * d_r)
        for plane, piece in enumerate(pieces):
            tail = jnp.zeros((8, width), F32)
            spread = pltpu.roll(jnp.concatenate([piece, tail], axis=0), skew, 0)
            spread = jnp.concatenate([spread, jnp.zeros((width + 8, wide - width), F32)], axis=1)
            grad[plane, rows, :] += pltpu.roll(spread, c, 1)
    parts = sums.shape[0]
    part = width // parts
    for p in range(parts):
        for q in range(6):
            half = slice((q % 2) * rim, (q % 2 + 1) * rim)
            sums[p, q * part : (q + 1) * part] = total[q // 2][p * part : (p + 1) * part, half]
    grad_a[...] = grad[:, lines[0]]
    grad_center[...] = grad[:, rim:foot]
    grad_b[...] = grad[:, lines[1]]


def scans(picks, rows_at, cols_at, count, odd, center, edges, probe, amps, parts):
    width = probe.shape[1]
    rim = width // 2
    th, tw = center.shape[1:]
    tall, wide = th + 2 * rim, tw + 2 * rim
    high, low = half_tables(width)
    smem = pl.BlockSpec(memory_space=pltpu.SMEM)
    vmem = pl.BlockSpec(memory_space=pltpu.VMEM)
    return pl.pallas_call(
        scan_kernel,
        in_specs=[smem] * 5 + [vmem] * 9,
        out_specs=[vmem] * 4,
        out_shape=[
            jax.ShapeDtypeStruct((2, rim, wide), F32),
            jax.ShapeDtypeStruct((2, th, wide), F32),
            jax.ShapeDtypeStruct((2, rim, wide), F32),
            jax.ShapeDtypeStruct((parts, 6 * width // parts, rim), F32),
        ],
        scratch_shapes=[pltpu.VMEM((2, tall, wide), F32), pltpu.VMEM((2, tall, wide), F32)],
        compiler_params=pltpu.CompilerParams(vmem_limit_bytes=VMEM_LIMIT),
        name="scan_step",
    )(picks, rows_at, cols_at, count, odd, center, *edges, probe, amps, high, low)


def piece_kernel(index, sums, probe, out):
    parts, rows, half = out.shape
    part = rows // 4
    at = pl.multiple_of(index[0] * part, part)
    for q in range(4):
        old = probe[q // 2, pl.ds(at, part), (q % 2) * half : (q % 2 + 1) * half]
        grad, light = sums[q * part : (q + 1) * part], sums[(4 + q % 2) * part : (5 + q % 2) * part]
        new = old + grad / (light + PROBE_REG)
        for p in range(parts):
            out[p, q * part : (q + 1) * part] = new


def probe_piece(sums, probe, parts, index):
    half = probe.shape[2] // 2
    vmem = pl.BlockSpec(memory_space=pltpu.VMEM)
    return pl.pallas_call(
        piece_kernel,
        in_specs=[pl.BlockSpec(memory_space=pltpu.SMEM), vmem, vmem],
        out_specs=vmem,
        out_shape=jax.ShapeDtypeStruct((parts, 4 * probe.shape[1] // parts, half), F32),
        compiler_params=pltpu.CompilerParams(vmem_limit_bytes=SMALL_VMEM),
        name="probe_piece",
    )(index.astype(jnp.int32).reshape(1), sums, probe)


def join_kernel(pieces, out):
    parts, rows, half = pieces.shape
    part = rows // 4
    for p in range(parts):
        for q in range(4):
            lanes = slice((q % 2) * half, (q % 2 + 1) * half)
            out[q // 2, p * part : (p + 1) * part, lanes] = pieces[p, q * part : (q + 1) * part]


def probe_joined(pieces, probe):
    vmem = pl.BlockSpec(memory_space=pltpu.VMEM)
    return pl.pallas_call(
        join_kernel,
        in_specs=[vmem],
        out_specs=vmem,
        out_shape=jax.ShapeDtypeStruct(probe.shape, F32),
        compiler_params=pltpu.CompilerParams(vmem_limit_bytes=SMALL_VMEM),
        name="probe_join",
    )(pieces)


def light_kernel(scans_at, probe, share, lit):
    width = probe.shape[1]
    rim = width // 2
    th, tw = share.shape
    wide = tw + 2 * rim
    lit[...] = jnp.zeros_like(lit)
    power = probe[0] * probe[0] + probe[1] * probe[1]
    power = jnp.concatenate([power, jnp.zeros((8, width), F32)], axis=0)
    power = jnp.concatenate([power, jnp.zeros((width + 8, wide - width), F32)], axis=1)
    for down in range(3):
        for right in range(3):
            for s in range(2):
                base = NOTE * (3 * down + right)

                @pl.when(s < scans_at[base + 10])
                def _():
                    j = base + scans_at[base + 8 + s]
                    r, c = scans_at[j], scans_at[j + 4]
                    skew = lax.rem(r, 8)
                    rows = pl.ds(pl.multiple_of(r - skew + down * th, 8), width + 8)
                    placed = pltpu.roll(pltpu.roll(power, skew, 0), c, 1)
                    lit[rows, right * tw : right * tw + wide] += placed

    share[...] = 1.0 / (lit[th + rim : 2 * th + rim, tw + rim : 2 * tw + rim] + OBJECT_REG)


def light_share(scans_at, probe, th, tw):
    width = probe.shape[1]
    rim = width // 2
    return pl.pallas_call(
        light_kernel,
        in_specs=[pl.BlockSpec(memory_space=pltpu.SMEM), pl.BlockSpec(memory_space=pltpu.VMEM)],
        out_specs=pl.BlockSpec(memory_space=pltpu.VMEM),
        out_shape=jax.ShapeDtypeStruct((th, tw), F32),
        scratch_shapes=[pltpu.VMEM((3 * th + 2 * rim, 3 * tw + 2 * rim), F32)],
        compiler_params=pltpu.CompilerParams(vmem_limit_bytes=SMALL_VMEM),
        cost_estimate=pl.CostEstimate(flops=20_000_000, bytes_accessed=1_000_000, transcendentals=0),
        name="light_share",
    )(scans_at, probe)


ROW = ("y_lo", "z_hi", "z_lo")
COL = ("y_hi", "x", "core")
NEAR = ("x", "core")
MID = ("y_lo", "y_hi")
SPLIT = {"y_lo": 4, "z_hi": 3, "z_lo": 4, "y_hi": 2, "x": 4, "core": 2}


def swaps(a, b, axis):
    peers = lax.axis_size(axis)

    def swap(part, start):
        pairs = [(i, i + 1) for i in range(start, peers - 1, 2)]
        return lax.ppermute(part, axis, pairs + [(j, i) for i, j in pairs])

    b = swap(b, 1)
    return swap(a, 0), b


def swapped(last, first, axis):
    odd = lax.axis_index(axis) % 2 == 1
    return swaps(jnp.where(odd, first, last), jnp.where(odd, last, first), axis)


def in_order(a, b, axis):
    odd = lax.axis_index(axis) % 2 == 1
    return jnp.where(odd, a, b), jnp.where(odd, b, a)


def exchanged(array, axes):
    return lax.all_to_all(array.reshape(lax.axis_size(axes), -1, array.shape[-1]), axes, 0, 0, tiled=True)


def copied(array, axes):
    return jnp.broadcast_to(array[None], (lax.axis_size(axes),) + array.shape)


def halo(object_field, note):
    rim = note.shape[0]
    th, tw = object_field.shape[1:]
    tail = jnp.broadcast_to(note, (2, TAIL, rim))

    def column(part):
        return jnp.concatenate([object_field[:, :, part], tail], axis=1)

    col_a, col_b = swapped(column(slice(tw - rim, tw)), column(slice(0, rim)), COL)

    def line(part):
        full = jnp.concatenate([col_a[:, part], object_field[:, part], col_b[:, part]], axis=2)
        notes = jnp.concatenate([col_a[:, th:], tail, tail, col_b[:, th:]], axis=2)
        return jnp.concatenate([full, notes], axis=1)

    row_a, row_b = swapped(line(slice(th - rim, th)), line(slice(0, rim)), ROW)
    left, right = in_order(col_a[0, th, :NOTE], col_b[0, th, :NOTE], COL)
    above, below = in_order(row_a[0, rim], row_b[0, rim], ROW)

    def three(row):
        near, far = in_order(row[:NOTE], row[rim + tw : rim + tw + NOTE], COL)
        return [near, row[rim : rim + NOTE], far]

    notes = three(above) + [left, note[:NOTE], right] + three(below)
    edges = (col_a, col_b, row_a, row_b)
    return edges, jnp.concatenate(notes).astype(jnp.int32)


def folded(grad, a, b):
    rim = a.shape[1]
    th = grad.shape[1]
    from_above, from_below = in_order(*swaps(a, b, ROW), ROW)
    grad = jnp.concatenate(
        [grad[:, :rim] + from_above, grad[:, rim : th - rim], grad[:, th - rim :] + from_below], axis=1
    )
    got = swapped(grad[:, :, -rim:], grad[:, :, :rim], COL)
    from_left, from_right = in_order(*got, COL)
    grad = grad[:, :, rim:-rim]
    return jnp.concatenate([grad[:, :, :rim] + from_left, grad[:, :, rim:] + from_right], axis=2)


def per_device(object_field, probe_field, amplitudes, pos_rows, pos_cols, scan_pick, scan_count):
    width = probe_field.shape[1]
    rim = width // 2
    th, tw = object_field.shape[1:]
    picks, rows_at, cols_at = scan_pick[0, 0], pos_rows[0, 0], pos_cols[0, 0]
    near = lax.axis_size(NEAR)
    own = jnp.concatenate([rows_at, cols_at, picks, scan_count])
    edges, scans_at = halo(object_field, jnp.pad(own.astype(F32), (0, rim - NOTE)))
    amps = ordered_amplitudes(amplitudes[0, 0], picks)
    odd = jnp.stack([lax.axis_index(ROW), lax.axis_index(COL)]).astype(jnp.int32) % 2
    above, grad, below, sums = scans(
        picks, rows_at, cols_at, scan_count, odd, object_field, edges, probe_field, amps, near
    )
    share = light_share(scans_at, probe_field, th, tw)
    mine = exchanged(sums, NEAR).sum(0)
    above, below, mine = lax.optimization_barrier((above, below, mine))
    mine = exchanged(mine, MID)
    share, mine = lax.optimization_barrier((share, mine))
    grad = folded(grad, above, below)
    mine = mine.sum(0)
    mine = exchanged(copied(mine, ("z_lo",)), ("z_lo",)).sum(0)
    mine = exchanged(copied(mine, ("z_hi",)), ("z_hi",)).sum(0)
    mine = exchanged(copied(mine, MID), MID).reshape(-1, rim)
    mine = exchanged(probe_piece(mine, probe_field, near, lax.axis_index(NEAR)), NEAR)
    return object_field + grad * share, probe_joined(mine, probe_field)


def solution(mesh):
    fine = Mesh(mesh.devices.reshape(tuple(SPLIT.values())), tuple(SPLIT))
    in_specs = (
        P(None, ROW, COL),
        P(),
        P(ROW, COL, None, None, None),
        P(ROW, COL, None),
        P(ROW, COL, None),
        P(ROW, COL, None),
        P(ROW + COL),
    )
    out_specs = (P(None, ROW, COL), P())

    return jax.shard_map(per_device, mesh=fine, in_specs=in_specs, out_specs=out_specs, check_vma=False)
```

```python
import math

import jax
import jax.numpy as jnp
import numpy as np
from jax import lax
from jax.experimental import pallas as pl
from jax.experimental.pallas import tpu as pltpu
from jax.sharding import Mesh
from jax.sharding import PartitionSpec as P


SOFTENING = 0.25
OBJECT_REG = 0.5
PROBE_REG = 1.0
F32, BF16 = jnp.float32, jnp.bfloat16
VMEM_LIMIT = 24 * 1024 * 1024
SMALL_VMEM = 10 * 1024 * 1024
NOTE = 11
TAIL = 8


def half_tables(width):
    half = width // 2
    n = np.arange(half)
    tables = []
    for odd in (0, 1):
        turn = ((2 * n[:, None] + odd) * n[None, :]) % width * (2.0 * np.pi / width)
        c, s = np.cos(turn) / math.sqrt(width), np.sin(turn) / math.sqrt(width)
        tables.append(np.block([[c, s], [-s, c]]))
    tables += [tables[0].T, tables[1].T]
    full = jnp.asarray(np.stack(tables), F32)
    high = full.astype(BF16)
    low = (full - high.astype(F32)).astype(BF16)
    return high, low


def sorting_table(width):
    order = np.concatenate([np.arange(0, width, 2), np.arange(1, width, 2)])
    return jnp.asarray(np.eye(width, dtype=np.float32)[order], BF16)


def dot(a, b):
    return lax.dot_general(a, b, (((1,), (0,)), ((), ())), preferred_element_type=F32)


def halves(x):
    high = x.astype(BF16)
    return high, (x - high.astype(F32)).astype(BF16)


def data_by_table(data, high, low):
    dh, dl = halves(data)
    return dot(dh, high) + (dot(dl, high) + dot(dh, low))


def table_by_data(high, low, data):
    dh, dl = halves(data)
    return dot(high, dh) + (dot(high, dl) + dot(low, dh))


def amplitude_kernel(pick, amps, order, out):
    ordered_rows = dot(order[...], amps[0]).astype(BF16)
    out[0] = lax.dot_general(
        ordered_rows, order[...], (((1,), (1,)), ((), ())), preferred_element_type=F32
    ).astype(BF16)


def ordered_amplitudes(amps, picks):
    slots, width = picks.shape[0], amps.shape[-1]
    return pl.pallas_call(
        amplitude_kernel,
        grid_spec=pltpu.PrefetchScalarGridSpec(
            num_scalar_prefetch=1,
            grid=(slots,),
            in_specs=[
                pl.BlockSpec((1, width, width), lambda s, pick: (pick[s], 0, 0)),
                pl.BlockSpec((width, width), lambda s, pick: (0, 0)),
            ],
            out_specs=pl.BlockSpec((1, width, width), lambda s, pick: (s, 0, 0)),
        ),
        out_shape=jax.ShapeDtypeStruct((slots, width, width), BF16),
        compiler_params=pltpu.CompilerParams(vmem_limit_bytes=SMALL_VMEM),
        name="amplitude_order",
    )(picks, amps, sorting_table(width))


def scan_kernel(
    pick, rows_at, cols_at, count, odd,
    center, col_a, col_b, row_a, row_b, probe, amps, high, low,
    grad_a, grad_center, grad_b, sums,
    ext, grad,
):
    width = probe.shape[1]
    rim = width // 2
    _, wide = ext.shape[1:]
    th, tw = center.shape[1:]
    slots = amps.shape[0]
    foot, side = rim + th, rim + tw
    lines = [pl.ds(pl.multiple_of(at, rim), rim) for at in (foot * (1 - odd[0]), foot * odd[0])]
    lanes = [pl.ds(pl.multiple_of(at, rim), rim) for at in (side * (1 - odd[1]), side * odd[1])]
    ext[:, rim:foot, rim:side] = center[...]
    for line, row in zip(lines, (row_a, row_b)):
        ext[:, line, rim:side] = row[:, :rim, rim:side]
        ext[:, line, lanes[0]] = row[:, :rim, :rim]
        ext[:, line, lanes[1]] = row[:, :rim, side:]
    ext[:, rim:foot, lanes[0]] = col_a[:, :th]
    ext[:, rim:foot, lanes[1]] = col_b[:, :th]
    grad[...] = jnp.zeros_like(grad)
    pr, pi = probe[0], probe[1]
    total = [jnp.zeros((width, width), F32) for _ in range(3)]
    for s in range(slots):
        j = pick[s]
        r, c = rows_at[j], cols_at[j]
        live = (s < count[0]).astype(F32)
        skew = lax.rem(r, 8)
        rows = pl.ds(pl.multiple_of(r - skew, 8), width + 8)
        up = lax.rem(width + 8 - skew, width + 8)
        back = lax.rem(wide - c, wide)

        def cut(plane):
            block = pltpu.roll(ext[plane, rows, :], back, 1)[:, :width]
            return pltpu.roll(block, up, 0)[:width]

        o_r, o_i = cut(0), cut(1)
        w_r, w_i = pr * o_r - pi * o_i, pr * o_i + pi * o_r
        even = jnp.concatenate([w_r[:rim] + w_r[rim:], w_i[:rim] + w_i[rim:]], axis=0)
        odd = jnp.concatenate([w_r[:rim] - w_r[rim:], w_i[:rim] - w_i[rim:]], axis=0)
        even = table_by_data(high[0], low[0], even)
        odd = table_by_data(high[1], low[1], odd)
        y_r = jnp.concatenate([even[:rim], odd[:rim]], axis=0)
        y_i = jnp.concatenate([even[rim:], odd[rim:]], axis=0)
        even = jnp.concatenate([y_r[:, :rim] + y_r[:, rim:], y_i[:, :rim] + y_i[:, rim:]], axis=1)
        odd = jnp.concatenate([y_r[:, :rim] - y_r[:, rim:], y_i[:, :rim] - y_i[:, rim:]], axis=1)
        even = data_by_table(even, high[2], low[2])
        odd = data_by_table(odd, high[3], low[3])
        m = amps[s].astype(F32)

        def weighted(z, m):
            re, im = z[:, :rim], z[:, rim:]
            weight = (m * lax.rsqrt(re * re + im * im + SOFTENING) - 1.0) * live
            return jnp.concatenate([re * weight, im * weight], axis=1)

        even = data_by_table(weighted(even, m[:, :rim]), high[0], low[0])
        odd = data_by_table(weighted(odd, m[:, rim:]), high[1], low[1])
        plus, minus = even + odd, even - odd
        y_r = jnp.concatenate([plus[:, :rim], minus[:, :rim]], axis=1)
        y_i = jnp.concatenate([plus[:, rim:], minus[:, rim:]], axis=1)
        even = table_by_data(high[2], low[2], jnp.concatenate([y_r[:rim], y_i[:rim]], axis=0))
        odd = table_by_data(high[3], low[3], jnp.concatenate([y_r[rim:], y_i[rim:]], axis=0))
        plus, minus = even + odd, even - odd
        d_r = jnp.concatenate([plus[:rim], minus[:rim]], axis=0)
        d_i = jnp.concatenate([plus[rim:], minus[rim:]], axis=0)
        total[0] += o_r * d_r + o_i * d_i
        total[1] += o_r * d_i - o_i * d_r
        total[2] += live * (o_r * o_r + o_i * o_i)
        pieces = (pr * d_r + pi * d_i, pr * d_i - pi * d_r)
        for plane, piece in enumerate(pieces):
            tail = jnp.zeros((8, width), F32)
            spread = pltpu.roll(jnp.concatenate([piece, tail], axis=0), skew, 0)
            spread = jnp.concatenate([spread, jnp.zeros((width + 8, wide - width), F32)], axis=1)
            grad[plane, rows, :] += pltpu.roll(spread, c, 1)
    parts = sums.shape[0]
    part = width // parts
    for p in range(parts):
        for q in range(6):
            half = slice((q % 2) * rim, (q % 2 + 1) * rim)
            sums[p, q * part : (q + 1) * part] = total[q // 2][p * part : (p + 1) * part, half]
    grad_a[...] = grad[:, lines[0]]
    grad_center[...] = grad[:, rim:foot]
    grad_b[...] = grad[:, lines[1]]


def scans(picks, rows_at, cols_at, count, odd, center, edges, probe, amps, parts):
    width = probe.shape[1]
    rim = width // 2
    th, tw = center.shape[1:]
    tall, wide = th + 2 * rim, tw + 2 * rim
    high, low = half_tables(width)
    smem = pl.BlockSpec(memory_space=pltpu.SMEM)
    vmem = pl.BlockSpec(memory_space=pltpu.VMEM)
    return pl.pallas_call(
        scan_kernel,
        in_specs=[smem] * 5 + [vmem] * 9,
        out_specs=[vmem] * 4,
        out_shape=[
            jax.ShapeDtypeStruct((2, rim, wide), F32),
            jax.ShapeDtypeStruct((2, th, wide), F32),
            jax.ShapeDtypeStruct((2, rim, wide), F32),
            jax.ShapeDtypeStruct((parts, 6 * width // parts, rim), F32),
        ],
        scratch_shapes=[pltpu.VMEM((2, tall, wide), F32), pltpu.VMEM((2, tall, wide), F32)],
        compiler_params=pltpu.CompilerParams(vmem_limit_bytes=VMEM_LIMIT),
        name="scan_step",
    )(picks, rows_at, cols_at, count, odd, center, *edges, probe, amps, high, low)


def piece_kernel(index, sums, probe, out):
    parts, rows, half = out.shape
    part = rows // 4
    at = pl.multiple_of(index[0] * part, part)
    for q in range(4):
        old = probe[q // 2, pl.ds(at, part), (q % 2) * half : (q % 2 + 1) * half]
        grad, light = sums[q * part : (q + 1) * part], sums[(4 + q % 2) * part : (5 + q % 2) * part]
        new = old + grad / (light + PROBE_REG)
        for p in range(parts):
            out[p, q * part : (q + 1) * part] = new


def probe_piece(sums, probe, parts, index):
    half = probe.shape[2] // 2
    vmem = pl.BlockSpec(memory_space=pltpu.VMEM)
    return pl.pallas_call(
        piece_kernel,
        in_specs=[pl.BlockSpec(memory_space=pltpu.SMEM), vmem, vmem],
        out_specs=vmem,
        out_shape=jax.ShapeDtypeStruct((parts, 4 * probe.shape[1] // parts, half), F32),
        compiler_params=pltpu.CompilerParams(vmem_limit_bytes=SMALL_VMEM),
        name="probe_piece",
    )(index.astype(jnp.int32).reshape(1), sums, probe)


def join_kernel(pieces, out):
    parts, rows, half = pieces.shape
    part = rows // 4
    for p in range(parts):
        for q in range(4):
            lanes = slice((q % 2) * half, (q % 2 + 1) * half)
            out[q // 2, p * part : (p + 1) * part, lanes] = pieces[p, q * part : (q + 1) * part]


def probe_joined(pieces, probe):
    vmem = pl.BlockSpec(memory_space=pltpu.VMEM)
    return pl.pallas_call(
        join_kernel,
        in_specs=[vmem],
        out_specs=vmem,
        out_shape=jax.ShapeDtypeStruct(probe.shape, F32),
        compiler_params=pltpu.CompilerParams(vmem_limit_bytes=SMALL_VMEM),
        name="probe_join",
    )(pieces)


def light_kernel(scans_at, probe, share, lit):
    width = probe.shape[1]
    rim = width // 2
    th, tw = share.shape
    wide = tw + 2 * rim
    lit[...] = jnp.zeros_like(lit)
    power = probe[0] * probe[0] + probe[1] * probe[1]
    power = jnp.concatenate([power, jnp.zeros((8, width), F32)], axis=0)
    power = jnp.concatenate([power, jnp.zeros((width + 8, wide - width), F32)], axis=1)
    for down in range(3):
        for right in range(3):
            for s in range(2):
                base = NOTE * (3 * down + right)

                @pl.when(s < scans_at[base + 10])
                def _():
                    j = base + scans_at[base + 8 + s]
                    r, c = scans_at[j], scans_at[j + 4]
                    skew = lax.rem(r, 8)
                    rows = pl.ds(pl.multiple_of(r - skew + down * th, 8), width + 8)
                    placed = pltpu.roll(pltpu.roll(power, skew, 0), c, 1)
                    lit[rows, right * tw : right * tw + wide] += placed

    share[...] = 1.0 / (lit[th + rim : 2 * th + rim, tw + rim : 2 * tw + rim] + OBJECT_REG)


def light_share(scans_at, probe, th, tw):
    width = probe.shape[1]
    rim = width // 2
    return pl.pallas_call(
        light_kernel,
        in_specs=[pl.BlockSpec(memory_space=pltpu.SMEM), pl.BlockSpec(memory_space=pltpu.VMEM)],
        out_specs=pl.BlockSpec(memory_space=pltpu.VMEM),
        out_shape=jax.ShapeDtypeStruct((th, tw), F32),
        scratch_shapes=[pltpu.VMEM((3 * th + 2 * rim, 3 * tw + 2 * rim), F32)],
        compiler_params=pltpu.CompilerParams(vmem_limit_bytes=SMALL_VMEM),
        cost_estimate=pl.CostEstimate(flops=20_000_000, bytes_accessed=1_000_000, transcendentals=0),
        name="light_share",
    )(scans_at, probe)


ROW = ("y_lo", "z_hi", "z_lo")
COL = ("y_hi", "x", "core")
NEAR = ("x", "core")
MID = ("y_lo", "y_hi")
SPLIT = {"y_lo": 4, "z_hi": 3, "z_lo": 4, "y_hi": 2, "x": 4, "core": 2}


def swaps(a, b, axis):
    peers = lax.axis_size(axis)

    def swap(part, start):
        pairs = [(i, i + 1) for i in range(start, peers - 1, 2)]
        return lax.ppermute(part, axis, pairs + [(j, i) for i, j in pairs])

    b = swap(b, 1)
    return swap(a, 0), b


def swapped(last, first, axis):
    odd = lax.axis_index(axis) % 2 == 1
    return swaps(jnp.where(odd, first, last), jnp.where(odd, last, first), axis)


def in_order(a, b, axis):
    odd = lax.axis_index(axis) % 2 == 1
    return jnp.where(odd, a, b), jnp.where(odd, b, a)


def exchanged(array, axes):
    return lax.all_to_all(array.reshape(lax.axis_size(axes), -1, array.shape[-1]), axes, 0, 0, tiled=True)


def copied(array, axes):
    return jnp.broadcast_to(array[None], (lax.axis_size(axes),) + array.shape)


def halo(object_field, note):
    rim = note.shape[0]
    th, tw = object_field.shape[1:]
    tail = jnp.broadcast_to(note, (2, TAIL, rim))

    def column(part):
        return jnp.concatenate([object_field[:, :, part], tail], axis=1)

    col_a, col_b = swapped(column(slice(tw - rim, tw)), column(slice(0, rim)), COL)

    def line(part):
        full = jnp.concatenate([col_a[:, part], object_field[:, part], col_b[:, part]], axis=2)
        notes = jnp.concatenate([col_a[:, th:], tail, tail, col_b[:, th:]], axis=2)
        return jnp.concatenate([full, notes], axis=1)

    row_a, row_b = swapped(line(slice(th - rim, th)), line(slice(0, rim)), ROW)
    left, right = in_order(col_a[0, th, :NOTE], col_b[0, th, :NOTE], COL)
    above, below = in_order(row_a[0, rim], row_b[0, rim], ROW)

    def three(row):
        near, far = in_order(row[:NOTE], row[rim + tw : rim + tw + NOTE], COL)
        return [near, row[rim : rim + NOTE], far]

    notes = three(above) + [left, note[:NOTE], right] + three(below)
    edges = (col_a, col_b, row_a, row_b)
    return edges, jnp.concatenate(notes).astype(jnp.int32)


def row_folded(grad, a, b):
    rim = a.shape[1]
    th = grad.shape[1]
    from_above, from_below = in_order(*swaps(a, b, ROW), ROW)
    return jnp.concatenate(
        [grad[:, :rim] + from_above, grad[:, rim : th - rim], grad[:, th - rim :] + from_below], axis=1
    )


def col_folded(grad, rim):
    got = swapped(grad[:, :, -rim:], grad[:, :, :rim], COL)
    from_left, from_right = in_order(*got, COL)
    grad = grad[:, :, rim:-rim]
    return jnp.concatenate([grad[:, :, :rim] + from_left, grad[:, :, rim:] + from_right], axis=2)


def per_device(object_field, probe_field, amplitudes, pos_rows, pos_cols, scan_pick, scan_count):
    width = probe_field.shape[1]
    rim = width // 2
    th, tw = object_field.shape[1:]
    picks, rows_at, cols_at = scan_pick[0, 0], pos_rows[0, 0], pos_cols[0, 0]
    near = lax.axis_size(NEAR)
    own = jnp.concatenate([rows_at, cols_at, picks, scan_count])
    edges, scans_at = halo(object_field, jnp.pad(own.astype(F32), (0, rim - NOTE)))
    amps = ordered_amplitudes(amplitudes[0, 0], picks)
    odd = jnp.stack([lax.axis_index(ROW), lax.axis_index(COL)]).astype(jnp.int32) % 2
    above, grad, below, sums = scans(
        picks, rows_at, cols_at, scan_count, odd, object_field, edges, probe_field, amps, near
    )
    share = light_share(scans_at, probe_field, th, tw)
    mine = exchanged(sums, NEAR)
    share, mine = lax.optimization_barrier((share, mine))
    mine = mine.sum(0)
    grad = row_folded(grad, above, below)
    mine = exchanged(mine, MID)
    grad, mine = lax.optimization_barrier((grad, mine))
    mine = mine.sum(0)
    grad = col_folded(grad, rim)
    mine = exchanged(copied(mine, ("z_lo",)), ("z_lo",)).sum(0)
    mine = exchanged(copied(mine, ("z_hi",)), ("z_hi",)).sum(0)
    mine = exchanged(copied(mine, MID), MID).reshape(-1, rim)
    mine = exchanged(probe_piece(mine, probe_field, near, lax.axis_index(NEAR)), NEAR)
    return object_field + grad * share, probe_joined(mine, probe_field)


def solution(mesh):
    fine = Mesh(mesh.devices.reshape(tuple(SPLIT.values())), tuple(SPLIT))
    in_specs = (
        P(None, ROW, COL),
        P(),
        P(ROW, COL, None, None, None),
        P(ROW, COL, None),
        P(ROW, COL, None),
        P(ROW, COL, None),
        P(ROW + COL),
    )
    out_specs = (P(None, ROW, COL), P())

    return jax.shard_map(per_device, mesh=fine, in_specs=in_specs, out_specs=out_specs, check_vma=False)
```

```python
import math

import jax
import jax.numpy as jnp
import numpy as np
from jax import lax
from jax.experimental import pallas as pl
from jax.experimental.pallas import tpu as pltpu
from jax.sharding import Mesh
from jax.sharding import PartitionSpec as P


SOFTENING = 0.25
OBJECT_REG = 0.5
PROBE_REG = 1.0
F32, BF16 = jnp.float32, jnp.bfloat16
VMEM_LIMIT = 24 * 1024 * 1024
SMALL_VMEM = 10 * 1024 * 1024
NOTE = 11
TAIL = 8


def half_tables(width):
    half = width // 2
    n = np.arange(half)
    tables = []
    for odd in (0, 1):
        turn = ((2 * n[:, None] + odd) * n[None, :]) % width * (2.0 * np.pi / width)
        c, s = np.cos(turn) / math.sqrt(width), np.sin(turn) / math.sqrt(width)
        tables.append(np.block([[c, s], [-s, c]]))
    tables += [tables[0].T, tables[1].T]
    full = jnp.asarray(np.stack(tables), F32)
    high = full.astype(BF16)
    low = (full - high.astype(F32)).astype(BF16)
    return high, low


def sorting_table(width):
    order = np.concatenate([np.arange(0, width, 2), np.arange(1, width, 2)])
    return jnp.asarray(np.eye(width, dtype=np.float32)[order], BF16)


def dot(a, b):
    return lax.dot_general(a, b, (((1,), (0,)), ((), ())), preferred_element_type=F32)


def halves(x):
    high = x.astype(BF16)
    return high, (x - high.astype(F32)).astype(BF16)


def data_by_table(data, high, low):
    dh, dl = halves(data)
    return dot(dh, high) + (dot(dl, high) + dot(dh, low))


def table_by_data(high, low, data):
    dh, dl = halves(data)
    return dot(high, dh) + (dot(high, dl) + dot(low, dh))


def amplitude_kernel(pick, amps, order, out):
    ordered_rows = dot(order[...], amps[0]).astype(BF16)
    out[0] = lax.dot_general(
        ordered_rows, order[...], (((1,), (1,)), ((), ())), preferred_element_type=F32
    ).astype(BF16)


def ordered_amplitudes(amps, picks):
    slots, width = picks.shape[0], amps.shape[-1]
    return pl.pallas_call(
        amplitude_kernel,
        grid_spec=pltpu.PrefetchScalarGridSpec(
            num_scalar_prefetch=1,
            grid=(slots,),
            in_specs=[
                pl.BlockSpec((1, width, width), lambda s, pick: (pick[s], 0, 0)),
                pl.BlockSpec((width, width), lambda s, pick: (0, 0)),
            ],
            out_specs=pl.BlockSpec((1, width, width), lambda s, pick: (s, 0, 0)),
        ),
        out_shape=jax.ShapeDtypeStruct((slots, width, width), BF16),
        compiler_params=pltpu.CompilerParams(vmem_limit_bytes=SMALL_VMEM),
        name="amplitude_order",
    )(picks, amps, sorting_table(width))


def scan_kernel(
    pick, rows_at, cols_at, count, odd,
    center, col_a, col_b, row_a, row_b, probe, amps, high, low,
    grad_a, grad_center, grad_b, sums,
    ext, grad,
):
    width = probe.shape[1]
    rim = width // 2
    _, wide = ext.shape[1:]
    th, tw = center.shape[1:]
    slots = amps.shape[0]
    foot, side = rim + th, rim + tw
    lines = [pl.ds(pl.multiple_of(at, rim), rim) for at in (foot * (1 - odd[0]), foot * odd[0])]
    lanes = [pl.ds(pl.multiple_of(at, rim), rim) for at in (side * (1 - odd[1]), side * odd[1])]
    ext[:, rim:foot, rim:side] = center[...]
    for line, row in zip(lines, (row_a, row_b)):
        ext[:, line, rim:side] = row[:, :rim, rim:side]
        ext[:, line, lanes[0]] = row[:, :rim, :rim]
        ext[:, line, lanes[1]] = row[:, :rim, side:]
    ext[:, rim:foot, lanes[0]] = col_a[:, :th]
    ext[:, rim:foot, lanes[1]] = col_b[:, :th]
    grad[...] = jnp.zeros_like(grad)
    pr, pi = probe[0], probe[1]
    total = [jnp.zeros((width, width), F32) for _ in range(3)]
    for s in range(slots):
        j = pick[s]
        r, c = rows_at[j], cols_at[j]
        live = (s < count[0]).astype(F32)
        skew = lax.rem(r, 8)
        rows = pl.ds(pl.multiple_of(r - skew, 8), width + 8)
        up = lax.rem(width + 8 - skew, width + 8)
        back = lax.rem(wide - c, wide)

        def cut(plane):
            block = pltpu.roll(ext[plane, rows, :], back, 1)[:, :width]
            return pltpu.roll(block, up, 0)[:width]

        o_r, o_i = cut(0), cut(1)
        w_r, w_i = pr * o_r - pi * o_i, pr * o_i + pi * o_r
        even = jnp.concatenate([w_r[:rim] + w_r[rim:], w_i[:rim] + w_i[rim:]], axis=0)
        odd = jnp.concatenate([w_r[:rim] - w_r[rim:], w_i[:rim] - w_i[rim:]], axis=0)
        even = table_by_data(high[0], low[0], even)
        odd = table_by_data(high[1], low[1], odd)
        y_r = jnp.concatenate([even[:rim], odd[:rim]], axis=0)
        y_i = jnp.concatenate([even[rim:], odd[rim:]], axis=0)
        even = jnp.concatenate([y_r[:, :rim] + y_r[:, rim:], y_i[:, :rim] + y_i[:, rim:]], axis=1)
        odd = jnp.concatenate([y_r[:, :rim] - y_r[:, rim:], y_i[:, :rim] - y_i[:, rim:]], axis=1)
        even = data_by_table(even, high[2], low[2])
        odd = data_by_table(odd, high[3], low[3])
        m = amps[s].astype(F32)

        def weighted(z, m):
            re, im = z[:, :rim], z[:, rim:]
            weight = (m * lax.rsqrt(re * re + im * im + SOFTENING) - 1.0) * live
            return jnp.concatenate([re * weight, im * weight], axis=1)

        even = data_by_table(weighted(even, m[:, :rim]), high[0], low[0])
        odd = data_by_table(weighted(odd, m[:, rim:]), high[1], low[1])
        plus, minus = even + odd, even - odd
        y_r = jnp.concatenate([plus[:, :rim], minus[:, :rim]], axis=1)
        y_i = jnp.concatenate([plus[:, rim:], minus[:, rim:]], axis=1)
        even = table_by_data(high[2], low[2], jnp.concatenate([y_r[:rim], y_i[:rim]], axis=0))
        odd = table_by_data(high[3], low[3], jnp.concatenate([y_r[rim:], y_i[rim:]], axis=0))
        plus, minus = even + odd, even - odd
        d_r = jnp.concatenate([plus[:rim], minus[:rim]], axis=0)
        d_i = jnp.concatenate([plus[rim:], minus[rim:]], axis=0)
        total[0] += o_r * d_r + o_i * d_i
        total[1] += o_r * d_i - o_i * d_r
        total[2] += live * (o_r * o_r + o_i * o_i)
        pieces = (pr * d_r + pi * d_i, pr * d_i - pi * d_r)
        for plane, piece in enumerate(pieces):
            tail = jnp.zeros((8, width), F32)
            spread = pltpu.roll(jnp.concatenate([piece, tail], axis=0), skew, 0)
            spread = jnp.concatenate([spread, jnp.zeros((width + 8, wide - width), F32)], axis=1)
            grad[plane, rows, :] += pltpu.roll(spread, c, 1)
    parts = sums.shape[0]
    part = width // parts
    for p in range(parts):
        for q in range(6):
            half = slice((q % 2) * rim, (q % 2 + 1) * rim)
            sums[p, q * part : (q + 1) * part] = total[q // 2][p * part : (p + 1) * part, half]
    grad_a[...] = grad[:, lines[0]]
    grad_center[...] = grad[:, rim:foot]
    grad_b[...] = grad[:, lines[1]]


def scans(picks, rows_at, cols_at, count, odd, center, edges, probe, amps, parts):
    width = probe.shape[1]
    rim = width // 2
    th, tw = center.shape[1:]
    tall, wide = th + 2 * rim, tw + 2 * rim
    high, low = half_tables(width)
    smem = pl.BlockSpec(memory_space=pltpu.SMEM)
    vmem = pl.BlockSpec(memory_space=pltpu.VMEM)
    return pl.pallas_call(
        scan_kernel,
        in_specs=[smem] * 5 + [vmem] * 9,
        out_specs=[vmem] * 4,
        out_shape=[
            jax.ShapeDtypeStruct((2, rim, wide), F32),
            jax.ShapeDtypeStruct((2, th, wide), F32),
            jax.ShapeDtypeStruct((2, rim, wide), F32),
            jax.ShapeDtypeStruct((parts, 6 * width // parts, rim), F32),
        ],
        scratch_shapes=[pltpu.VMEM((2, tall, wide), F32), pltpu.VMEM((2, tall, wide), F32)],
        compiler_params=pltpu.CompilerParams(vmem_limit_bytes=VMEM_LIMIT),
        name="scan_step",
    )(picks, rows_at, cols_at, count, odd, center, *edges, probe, amps, high, low)


def piece_kernel(index, sums, probe, out):
    parts, rows, half = out.shape
    part = rows // 4
    at = pl.multiple_of(index[0] * part, part)
    for q in range(4):
        old = probe[q // 2, pl.ds(at, part), (q % 2) * half : (q % 2 + 1) * half]
        grad, light = sums[q * part : (q + 1) * part], sums[(4 + q % 2) * part : (5 + q % 2) * part]
        new = old + grad / (light + PROBE_REG)
        for p in range(parts):
            out[p, q * part : (q + 1) * part] = new


def probe_piece(sums, probe, parts, index):
    half = probe.shape[2] // 2
    vmem = pl.BlockSpec(memory_space=pltpu.VMEM)
    return pl.pallas_call(
        piece_kernel,
        in_specs=[pl.BlockSpec(memory_space=pltpu.SMEM), vmem, vmem],
        out_specs=vmem,
        out_shape=jax.ShapeDtypeStruct((parts, 4 * probe.shape[1] // parts, half), F32),
        compiler_params=pltpu.CompilerParams(vmem_limit_bytes=SMALL_VMEM),
        name="probe_piece",
    )(index.astype(jnp.int32).reshape(1), sums, probe)


def join_kernel(pieces, out):
    parts, rows, half = pieces.shape
    part = rows // 4
    for p in range(parts):
        for q in range(4):
            lanes = slice((q % 2) * half, (q % 2 + 1) * half)
            out[q // 2, p * part : (p + 1) * part, lanes] = pieces[p, q * part : (q + 1) * part]


def probe_joined(pieces, probe):
    vmem = pl.BlockSpec(memory_space=pltpu.VMEM)
    return pl.pallas_call(
        join_kernel,
        in_specs=[vmem],
        out_specs=vmem,
        out_shape=jax.ShapeDtypeStruct(probe.shape, F32),
        compiler_params=pltpu.CompilerParams(vmem_limit_bytes=SMALL_VMEM),
        name="probe_join",
    )(pieces)


def relay_kernel(parts, out):
    total = parts[0]
    for p in range(1, parts.shape[0]):
        total = total + parts[p]
    for p in range(out.shape[0]):
        out[p] = total


def relayed(parts, axes):
    vmem = pl.BlockSpec(memory_space=pltpu.VMEM)
    return pl.pallas_call(
        relay_kernel,
        in_specs=[vmem],
        out_specs=vmem,
        out_shape=jax.ShapeDtypeStruct((lax.axis_size(axes),) + parts.shape[1:], F32),
        compiler_params=pltpu.CompilerParams(vmem_limit_bytes=SMALL_VMEM),
        name="relay",
    )(parts)


def light_kernel(scans_at, probe, share, lit):
    width = probe.shape[1]
    rim = width // 2
    th, tw = share.shape
    wide = tw + 2 * rim
    lit[...] = jnp.zeros_like(lit)
    power = probe[0] * probe[0] + probe[1] * probe[1]
    power = jnp.concatenate([power, jnp.zeros((8, width), F32)], axis=0)
    power = jnp.concatenate([power, jnp.zeros((width + 8, wide - width), F32)], axis=1)
    for down in range(3):
        for right in range(3):
            for s in range(2):
                base = NOTE * (3 * down + right)

                @pl.when(s < scans_at[base + 10])
                def _():
                    j = base + scans_at[base + 8 + s]
                    r, c = scans_at[j], scans_at[j + 4]
                    skew = lax.rem(r, 8)
                    rows = pl.ds(pl.multiple_of(r - skew + down * th, 8), width + 8)
                    placed = pltpu.roll(pltpu.roll(power, skew, 0), c, 1)
                    lit[rows, right * tw : right * tw + wide] += placed

    share[...] = 1.0 / (lit[th + rim : 2 * th + rim, tw + rim : 2 * tw + rim] + OBJECT_REG)


def light_share(scans_at, probe, th, tw):
    width = probe.shape[1]
    rim = width // 2
    return pl.pallas_call(
        light_kernel,
        in_specs=[pl.BlockSpec(memory_space=pltpu.SMEM), pl.BlockSpec(memory_space=pltpu.VMEM)],
        out_specs=pl.BlockSpec(memory_space=pltpu.VMEM),
        out_shape=jax.ShapeDtypeStruct((th, tw), F32),
        scratch_shapes=[pltpu.VMEM((3 * th + 2 * rim, 3 * tw + 2 * rim), F32)],
        compiler_params=pltpu.CompilerParams(vmem_limit_bytes=SMALL_VMEM),
        cost_estimate=pl.CostEstimate(flops=20_000_000, bytes_accessed=1_000_000, transcendentals=0),
        name="light_share",
    )(scans_at, probe)


ROW = ("y_lo", "z_hi", "z_lo")
COL = ("y_hi", "x", "core")
NEAR = ("x", "core")
MID = ("y_lo", "y_hi")
SPLIT = {"y_lo": 4, "z_hi": 3, "z_lo": 4, "y_hi": 2, "x": 4, "core": 2}


def swaps(a, b, axis):
    peers = lax.axis_size(axis)

    def swap(part, start):
        pairs = [(i, i + 1) for i in range(start, peers - 1, 2)]
        return lax.ppermute(part, axis, pairs + [(j, i) for i, j in pairs])

    b = swap(b, 1)
    return swap(a, 0), b


def swapped(last, first, axis):
    odd = lax.axis_index(axis) % 2 == 1
    return swaps(jnp.where(odd, first, last), jnp.where(odd, last, first), axis)


def in_order(a, b, axis):
    odd = lax.axis_index(axis) % 2 == 1
    return jnp.where(odd, a, b), jnp.where(odd, b, a)


def exchanged(array, axes):
    return lax.all_to_all(array.reshape(lax.axis_size(axes), -1, array.shape[-1]), axes, 0, 0, tiled=True)


def halo(object_field, note):
    rim = note.shape[0]
    th, tw = object_field.shape[1:]
    tail = jnp.broadcast_to(note, (2, TAIL, rim))

    def column(part):
        return jnp.concatenate([object_field[:, :, part], tail], axis=1)

    col_a, col_b = swapped(column(slice(tw - rim, tw)), column(slice(0, rim)), COL)

    def line(part):
        full = jnp.concatenate([col_a[:, part], object_field[:, part], col_b[:, part]], axis=2)
        notes = jnp.concatenate([col_a[:, th:], tail, tail, col_b[:, th:]], axis=2)
        return jnp.concatenate([full, notes], axis=1)

    row_a, row_b = swapped(line(slice(th - rim, th)), line(slice(0, rim)), ROW)
    left, right = in_order(col_a[0, th, :NOTE], col_b[0, th, :NOTE], COL)
    above, below = in_order(row_a[0, rim], row_b[0, rim], ROW)

    def three(row):
        near, far = in_order(row[:NOTE], row[rim + tw : rim + tw + NOTE], COL)
        return [near, row[rim : rim + NOTE], far]

    notes = three(above) + [left, note[:NOTE], right] + three(below)
    edges = (col_a, col_b, row_a, row_b)
    return edges, jnp.concatenate(notes).astype(jnp.int32)


def row_folded(grad, a, b):
    rim = a.shape[1]
    th = grad.shape[1]
    from_above, from_below = in_order(*swaps(a, b, ROW), ROW)
    return jnp.concatenate(
        [grad[:, :rim] + from_above, grad[:, rim : th - rim], grad[:, th - rim :] + from_below], axis=1
    )


def col_folded(grad, rim):
    got = swapped(grad[:, :, -rim:], grad[:, :, :rim], COL)
    from_left, from_right = in_order(*got, COL)
    grad = grad[:, :, rim:-rim]
    return jnp.concatenate([grad[:, :, :rim] + from_left, grad[:, :, rim:] + from_right], axis=2)


def per_device(object_field, probe_field, amplitudes, pos_rows, pos_cols, scan_pick, scan_count):
    width = probe_field.shape[1]
    rim = width // 2
    th, tw = object_field.shape[1:]
    picks, rows_at, cols_at = scan_pick[0, 0], pos_rows[0, 0], pos_cols[0, 0]
    near = lax.axis_size(NEAR)
    own = jnp.concatenate([rows_at, cols_at, picks, scan_count])
    edges, scans_at = halo(object_field, jnp.pad(own.astype(F32), (0, rim - NOTE)))
    amps = ordered_amplitudes(amplitudes[0, 0], picks)
    odd = jnp.stack([lax.axis_index(ROW), lax.axis_index(COL)]).astype(jnp.int32) % 2
    above, grad, below, sums = scans(
        picks, rows_at, cols_at, scan_count, odd, object_field, edges, probe_field, amps, near
    )
    share = light_share(scans_at, probe_field, th, tw)
    mine = exchanged(sums, NEAR)
    share, mine = lax.optimization_barrier((share, mine))
    mine = mine.sum(0)
    grad = row_folded(grad, above, below)
    mine = exchanged(mine, MID)
    grad, mine = lax.optimization_barrier((grad, mine))
    grad = col_folded(grad, rim)
    mine = exchanged(relayed(mine, ("z_lo",)), ("z_lo",))
    mine = exchanged(relayed(mine, ("z_hi",)), ("z_hi",))
    mine = exchanged(relayed(mine, MID), MID).reshape(-1, rim)
    mine = exchanged(probe_piece(mine, probe_field, near, lax.axis_index(NEAR)), NEAR)
    return object_field + grad * share, probe_joined(mine, probe_field)


def solution(mesh):
    fine = Mesh(mesh.devices.reshape(tuple(SPLIT.values())), tuple(SPLIT))
    in_specs = (
        P(None, ROW, COL),
        P(),
        P(ROW, COL, None, None, None),
        P(ROW, COL, None),
        P(ROW, COL, None),
        P(ROW, COL, None),
        P(ROW + COL),
    )
    out_specs = (P(None, ROW, COL), P())

    return jax.shard_map(per_device, mesh=fine, in_specs=in_specs, out_specs=out_specs, check_vma=False)
```
